32 devices in a mesh: clus: 8 (over y, x, core), col: 4 (over z).
Axes of the slice: x: 2, y: 2, z: 4, core: 2. Of those that a mesh axis runs over, the one named last changes fastest.
Arguments:
- density: bfloat16 [4096, 4096], P('clus', 'col'), may hold values from -6 to 6
- dens_pattern: int32 [16, 16], P('clus', 'col'), may hold values 0 or 1
- margin_window: bfloat16 [4096, 2048], P('col', 'clus'), may hold values from -0.09375 to 0.09375
- ovl_pattern: int32 [16, 8], P('col', 'clus'), may hold values 0 or 1
- keep_mask: int32 [8, 8], P('clus', 'col'), may hold values 0 or 1
- basis_values: bfloat16 [16, 256, 4096], P('col'), may hold values from -0.375 to 0.375
- rest_density: float32 [256, 256, 256], P('clus', 'col'), may hold values from -0.6 to 0.6
- slab_owner: int32 [16], replicated, may hold values from 0 to 7
- cell_lengths: float32 [3], replicated, may hold values from 200 to 260
Outputs:
- potential: float32 [256, 256, 256], P('clus', 'col')
- hartree: bfloat16 [4096, 4096], P('clus', 'col')
- product: bfloat16 [2048, 2048], P('clus', 'col')
The draws below stay inside these ranges and needn't reach their ends.
All inputs are finite; a program needn't handle non-finite values. No bound on the sum of `dens_pattern` or of `ovl_pattern` or of `keep_mask` on one device may be relied on, other than what follows from the above.
Results may differ from the reference program's by a relative error of at most 0.0049.
Values may be sent and summed in bfloat16 or wider, within the bound.
No kernel may reach another device: no remote copies, remote signals or barrier semaphores. Data moves between devices by JAX's collectives and lax.ppermute only.
A program may use at most 128 MiB of HBM per device.

```python
import math
import jax
import jax.numpy as jnp
import numpy as np
from jax import lax

B = 256
G = 256
BR_DEV = 2
PATCH_Y = 32
QZ = 128
NB = 16
M = 4096
WIN = 2048
PATCH = 4096
N_CLUS = 8
N_COL = 4


def place_ends(result, rng, low, high):
    dims = result.shape
    index_at = [jax.random.randint(jax.random.fold_in(rng, axis), (), 0, dims[axis]) for axis in range(len(dims))]
    result = result.at[tuple(index_at)].set(low)
    longest = dims.index(max(dims))
    index_at[longest] = (index_at[longest] + 1) % dims[longest]
    return result.at[tuple(index_at)].set(high)


def block_levels(rng, extent, split, smallest, high):
    factor_of, own = 1.0, jax.random.fold_in(rng, 6)
    for axis_at, parts in split:
        heights = jnp.exp(jax.random.uniform(jax.random.fold_in(own, axis_at), (parts,), jnp.float32, smallest / len(split), high / len(split)))
        factor_of = factor_of * jnp.repeat(heights, extent[axis_at] // parts).reshape([-1 if axis == axis_at else 1 for axis in range(len(extent))])
    return factor_of


def rank_bounds(count, skew):
    portions = [(1 << 20) // math.isqrt(standing ** skew) + 1 for standing in range(1, count + 1)]
    width = 1 + sum(portions) // (1 << 30)
    return np.cumsum(np.array([max(1, weight // width) for weight in portions]))


def ranked_ids(rng, extent, amount, slope):
    listing = rank_bounds(amount, slope)
    pick = jax.random.randint(jax.random.fold_in(rng, 1), extent, 0, int(listing[amount - 1]))
    grade = jnp.searchsorted(jnp.asarray(listing, jnp.int32), pick, side="right")
    return jax.random.permutation(jax.random.fold_in(rng, 2), amount)[grade].astype(jnp.int32)


def bell_draw(rng, extent, scale, limit, cuts=(), kind=jnp.bfloat16):
    values = scale * jax.random.normal(rng, extent, jnp.float32)
    if cuts:
        values = values * block_levels(rng, extent, cuts, -0.22, 0.18)
    return jnp.clip(values, -limit, limit).astype(kind)


def setup_inputs(seed: int = 0) -> dict:
    key_of = jax.random.split(jax.random.key(seed), 10)
    return {
        "density": bell_draw(key_of[0], (M, M), 1.0, 6.0, ((0, 8), (1, 4))),
        "dens_pattern": place_ends((jax.random.randint(key_of[1], (NB, NB), 0, 2) < 1).astype(jnp.int32), jax.random.fold_in(key_of[1], 1), 0, 1),
        "margin_window": bell_draw(key_of[2], (M, WIN), M ** -0.5, 0.09375, ((0, 4), (1, 8))),
        "ovl_pattern": place_ends((jax.random.randint(key_of[3], (NB, N_CLUS), 0, 2) < 1).astype(jnp.int32), jax.random.fold_in(key_of[3], 1), 0, 1),
        "keep_mask": place_ends((jax.random.randint(key_of[4], (N_CLUS, N_CLUS), 0, 4) < 3).astype(jnp.int32), jax.random.fold_in(key_of[4], 1), 0, 1),
        "basis_values": bell_draw(key_of[5], (NB, B, PATCH), B ** -0.5, 0.375, ((0, 4),)),
        "rest_density": bell_draw(key_of[6], (G, G, G), 0.1, 0.6, ((0, 8), (1, 4)), jnp.float32),
        "slab_owner": place_ends(ranked_ids(key_of[7], (NB,), N_CLUS, 2), jax.random.fold_in(key_of[7], 3), 0, N_CLUS - 1).astype(jnp.int32),
        "cell_lengths": jnp.clip(jax.random.uniform(key_of[8], (3,), jnp.float32, 200.0, 260.0), 200.0, 260.0),
    }


four_pi = 4.0 * math.pi


def green_values(cell_lengths, freq_x, freq_y, freq_z):
    def squared_wave(frequency, axis_pos):
        signed = jnp.where(frequency < G // 2, frequency, frequency - G).astype(jnp.float32)
        scaled = signed * (2.0 * math.pi) / cell_lengths[axis_pos]
        return scaled * scaled

    squared = squared_wave(freq_x, 0) + squared_wave(freq_y, 1) + squared_wave(freq_z, 2)
    at_anchor = (freq_x == 0) & (freq_y == 0) & (freq_z == 0)
    return jnp.where(at_anchor, 0.0, four_pi / jnp.where(at_anchor, 1.0, squared))


def reference(density, dens_pattern, margin_window, ovl_pattern, keep_mask, basis_values, rest_density, slab_owner, cell_lengths):
    masked = (density.reshape(NB, B, NB, B) * dens_pattern.astype(jnp.bfloat16)[:, None, :, None]).reshape(M, M)
    window_rows = masked.reshape(N_CLUS, BR_DEV * B, M)[:, :B].reshape(WIN, M)
    margin_masked = (margin_window.reshape(NB, B, N_CLUS, B) * ovl_pattern.astype(jnp.bfloat16)[:, None, :, None]).reshape(M, WIN)
    summed = jnp.dot(window_rows, margin_masked, preferred_element_type=jnp.float32)
    product = (summed.reshape(N_CLUS, B, N_CLUS, B) * keep_mask.astype(jnp.float32)[:, None, :, None]).reshape(WIN, WIN).astype(jnp.bfloat16)
    phi_stack = basis_values.reshape(M, PATCH)
    lifted = jnp.dot(masked, phi_stack, preferred_element_type=jnp.float32)
    patch_rho = jnp.sum(basis_values.astype(jnp.float32) * lifted.reshape(NB, B, PATCH), axis=1)
    block_ids = jnp.arange(NB, dtype=jnp.int32)
    plane_count = G // N_CLUS
    line_count = G // N_COL
    lines_dev = PATCH_Y // N_COL
    x_cells = slab_owner.astype(jnp.int32) * plane_count + block_ids % plane_count
    col_lines = jnp.arange(N_COL, dtype=jnp.int32)[:, None] * line_count + jnp.arange(lines_dev, dtype=jnp.int32)[None, :]
    y_cells = col_lines[None, :, :] + ((block_ids // plane_count) * lines_dev)[:, None, None]
    z_cells = (G - QZ) // 2 + jnp.arange(QZ, dtype=jnp.int32)
    index_x = x_cells[:, None, None, None]
    index_y = y_cells[:, :, :, None]
    index_z = z_cells[None, None, None, :]
    placed = jnp.zeros((G, G, G), jnp.float32).at[index_x, index_y, index_z].add(patch_rho.reshape(NB, N_COL, lines_dev, QZ))
    density_grid = rest_density + placed
    frequency = jnp.arange(G, dtype=jnp.int32)
    green_table = green_values(cell_lengths, frequency[:, None, None], frequency[None, :, None], frequency[None, None, :])
    spectrum = jnp.fft.fftn(density_grid) * green_table
    potential = jnp.real(jnp.fft.ifftn(spectrum)).astype(jnp.float32)
    patch_pot = potential[index_x, index_y, index_z].reshape(NB, PATCH)
    weighted = (basis_values.astype(jnp.float32) * patch_pot[:, None, :]).astype(jnp.bfloat16)
    pattern_float = dens_pattern.astype(jnp.float32)

    def one_row(inputs):
        rows_bf, pattern_row = inputs
        full_row = lax.dot_general(rows_bf, phi_stack, (((1,), (1,)), ((), ())), preferred_element_type=jnp.float32)
        return (full_row.reshape(B, NB, B) * pattern_row[None, :, None]).reshape(B, M).astype(jnp.bfloat16)

    hartree = lax.map(one_row, (weighted, pattern_float)).reshape(M, M)
    return potential, hartree, product
```

```python
import math

import jax
import jax.numpy as jnp
import numpy as np
from jax import lax
from jax.experimental import pallas as pl
from jax.experimental.pallas import tpu as pltpu
from jax.sharding import PartitionSpec as P


QZ = 128
AXES = ("clus", "col")
HIGH = lax.Precision.HIGH


def cas_table(size):
    counter = np.arange(size)
    angles = (counter[:, None] * counter[None, :] % size) * (2.0 * math.pi / size)
    return (np.cos(angles) + np.sin(angles)).astype(np.float32)


def dot_high(equation, left_side, right_side):
    return jnp.einsum(
        equation, left_side, right_side, precision=HIGH, preferred_element_type=jnp.float32
    )


def exchange(values):
    return lax.all_to_all(values, AXES, split_axis=0, concat_axis=0, tiled=True)


def green_planes(cell_lengths, size, first, depth):
    def squared_wave(frequency, axis_pos):
        signed = jnp.where(frequency < size // 2, frequency, frequency - size).astype(jnp.float32)
        scaled = signed * (2.0 * math.pi) / cell_lengths[axis_pos]
        return scaled * scaled

    freq_z = first + jnp.arange(depth, dtype=jnp.int32)[:, None, None]
    freq_x = jnp.arange(size, dtype=jnp.int32)[None, :, None]
    freq_y = jnp.arange(size, dtype=jnp.int32)[None, None, :]
    squared = squared_wave(freq_x, 0) + squared_wave(freq_y, 1) + squared_wave(freq_z, 2)
    at_anchor = (freq_x == 0) & (freq_y == 0) & (freq_z == 0)
    return jnp.where(at_anchor, 0.0, 4.0 * math.pi / jnp.where(at_anchor, 1.0, squared))


def after(values, *others):
    return lax.optimization_barrier((values,) + others)[0]


def lift_kernel(order_ref, basis_ref, margin_ref, *refs, count):
    part_refs, lifted_ref, window_ref, held = refs[:count], refs[count], refs[count + 1], refs[count + 2]
    step = pl.program_id(0)
    for e in range(count):

        @pl.when(step == e)
        def _(e=e):
            held[...] = part_refs[e][...]

    block = margin_ref.shape[1]
    window_ref[0] = jnp.dot(
        held[:block, :], margin_ref[...], preferred_element_type=jnp.float32
    )

    @pl.loop(0, held.shape[0] // block)
    def _(i):
        at = pl.ds(pl.multiple_of(i * block, block), block)
        lifted_ref[0, at, :] = jnp.dot(
            held[at, :], basis_ref[...], preferred_element_type=jnp.float32
        )


def lift(order, basis, margin, parts):
    count = len(parts)
    height, depth = parts[0].shape
    width, block = basis.shape[1], margin.shape[1]
    once = pl.Buffered(1)
    whole = lambda i, s: (0, 0)
    return pl.pallas_call(
        lambda *refs: lift_kernel(*refs, count=count),
        out_shape=[
            jax.ShapeDtypeStruct((count, height, width), jnp.float32),
            jax.ShapeDtypeStruct((count, block, block), jnp.float32),
        ],
        grid_spec=pltpu.PrefetchScalarGridSpec(
            num_scalar_prefetch=1,
            grid=(count,),
            in_specs=[
                pl.BlockSpec((depth, width), whole, pipeline_mode=once),
                pl.BlockSpec((depth, block), whole, pipeline_mode=once),
            ]
            + [pl.BlockSpec((height, depth), whole, pipeline_mode=once) for _ in parts],
            out_specs=[
                pl.BlockSpec((1, height, width), lambda i, s: (s[i], 0, 0)),
                pl.BlockSpec((1, block, block), lambda i, s: (s[i], 0, 0)),
            ],
            scratch_shapes=[pltpu.VMEM((height, depth), jnp.bfloat16)],
        ),
        cost_estimate=pl.CostEstimate(
            flops=2 * height * depth * width * count,
            bytes_accessed=count * (2 * height * depth + 4 * height * width),
            transcendentals=0,
        ),
        name="lift",
    )(order, basis, margin, *parts)


def route_kernel(owner_ref, where_ref, part_ref, lifted_ref, *refs, pieces, outs):
    piece_refs, out_refs = refs[:pieces], refs[pieces : pieces + outs]
    rho_ref, held, in_sems, out_sems = refs[pieces + outs :]
    rows = held.shape[1]
    step = pl.program_id(0)

    @pl.when(step == 0)
    def _():
        for e in range(outs):
            start = part_ref[e] * rows
            for p in range(pieces):

                @pl.when(where_ref[e] == p)
                def _(e=e, p=p, start=start):
                    pltpu.make_async_copy(
                        piece_refs[p].at[pl.ds(start, rows)], held.at[e], in_sems.at[e]
                    ).start()

    pltpu.make_async_copy(
        piece_refs[0].at[pl.ds(0, rows)], held.at[step], in_sems.at[step]
    ).wait()
    for e in range(outs):

        @pl.when(step == e)
        def _(e=e):
            pltpu.make_async_copy(held.at[e], out_refs[e], out_sems.at[e]).start()

    for b in range(rows):
        basis = held[step, b].astype(jnp.float32)
        height = basis.shape[0]
        rho_ref[0, b : b + 1, :] = jnp.sum(
            basis * lifted_ref[0, b * height : (b + 1) * height, :], axis=0, keepdims=True
        )

    @pl.when(step == outs - 1)
    def _():
        for e in range(outs):
            pltpu.make_async_copy(held.at[e], out_refs[e], out_sems.at[e]).wait()


def route(owner, where, part, lifted, pieces, rows):
    outs = where.shape[0]
    shape = (rows,) + pieces[0].shape[1:]
    height, width = lifted.shape[1:]
    size = math.prod(shape) * outs
    return pl.pallas_call(
        lambda *refs: route_kernel(*refs, pieces=len(pieces), outs=outs),
        out_shape=[jax.ShapeDtypeStruct(shape, pieces[0].dtype)] * outs
        + [jax.ShapeDtypeStruct((outs, rows, width), jnp.float32)],
        grid_spec=pltpu.PrefetchScalarGridSpec(
            num_scalar_prefetch=3,
            grid=(outs,),
            in_specs=[pl.BlockSpec((1, height, width), lambda i, o, w, p: (o[i], 0, 0))]
            + [pl.BlockSpec(memory_space=pl.ANY)] * len(pieces),
            out_specs=[pl.BlockSpec(memory_space=pl.ANY)] * outs
            + [pl.BlockSpec((1, rows, width), lambda i, o, w, p: (o[i], 0, 0))],
            scratch_shapes=[
                pltpu.VMEM((outs,) + shape, pieces[0].dtype),
                pltpu.SemaphoreType.DMA((outs,)),
                pltpu.SemaphoreType.DMA((outs,)),
            ],
        ),
        cost_estimate=pl.CostEstimate(
            flops=2 * size, bytes_accessed=4 * size + 4 * size, transcendentals=0
        ),
        name="route",
    )(owner, where, part, lifted, *pieces)


def hartree_kernel(slot_ref, pattern_ref, pot_ref, columns_ref, *refs, count):
    row_refs, out_ref, scaled = refs[:count], refs[count], refs[count + 1]
    step = pl.program_id(0)
    rows, block, width = row_refs[0].shape

    @pl.when(step == 0)
    def _():
        for e in range(count):
            at = pl.ds(pl.multiple_of(slot_ref[e] * width, width), width)
            for b in range(rows):
                scaled[pl.ds(b * block, block), at] = (
                    row_refs[e][b].astype(jnp.float32) * pot_ref[b : b + 1, at]
                ).astype(jnp.bfloat16)

    @pl.loop(0, rows)
    def _(b):
        at = pl.ds(pl.multiple_of(b * block, block), block)
        keep = pattern_ref[b, step].astype(jnp.float32)
        values = lax.dot_general(
            scaled[at, :],
            columns_ref[...],
            (((1,), (1,)), ((), ())),
            preferred_element_type=jnp.float32,
        )
        out_ref[at, :] = (values * keep).astype(jnp.bfloat16)


def hartree_product(slots, pattern, pot, columns, row_parts):
    count = len(row_parts)
    rows, block, width = row_parts[0].shape
    depth, cells = columns.shape
    height = rows * block
    once = pl.Buffered(1)
    return pl.pallas_call(
        lambda *refs: hartree_kernel(*refs, count=count),
        out_shape=jax.ShapeDtypeStruct((height, depth), jnp.bfloat16),
        grid_spec=pltpu.PrefetchScalarGridSpec(
            num_scalar_prefetch=2,
            grid=(depth // block,),
            in_specs=[
                pl.BlockSpec(pot.shape, lambda i, s, p: (0, 0), pipeline_mode=once),
                pl.BlockSpec((block, cells), lambda i, s, p: (i, 0)),
            ]
            + [
                pl.BlockSpec((rows, block, width), lambda i, s, p: (0, 0, 0), pipeline_mode=once)
                for _ in row_parts
            ],
            out_specs=pl.BlockSpec((height, block), lambda i, s, p: (0, i)),
            scratch_shapes=[pltpu.VMEM((height, cells), jnp.bfloat16)],
        ),
        cost_estimate=pl.CostEstimate(
            flops=2 * height * depth * cells,
            bytes_accessed=2 * (depth + height) * cells,
            transcendentals=0,
        ),
        name="hartree",
    )(slots, pattern, pot, columns, *row_parts)


def make_program(clus_count, col_count):
    def pairs(move):
        return [
            (k * col_count + c, k2 * col_count + c2)
            for k in range(clus_count)
            for c in range(col_count)
            for k2, c2 in [move(k, c)]
            if 0 <= c2 < col_count
        ]

    def swap(values, distance):
        return lax.ppermute(values, AXES, pairs(lambda k, c: (k ^ distance, c)))

    even = [c ^ 1 for c in range(col_count)]
    odd = [c if c in (0, col_count - 1) else c - 1 if c % 2 == 0 else c + 1 for c in range(col_count)]
    moves = []
    holds = [list(range(col_count))]
    tips = [0, 0]
    while any(len({h[c] for h in holds}) < col_count for c in range(col_count)):
        made = []
        for kind, table in enumerate((even, odd)):
            arrived = [holds[tips[kind]][table[c]] for c in range(col_count)]
            if all(arrived[c] in [h[c] for h in holds] for c in range(col_count)):
                made.append(None)
                continue
            moves.append((kind, tips[kind]))
            holds.append(arrived)
            made.append(len(holds) - 1)
        tips = [made[1], made[0]]
    place = np.array(
        [[[h[c] for h in holds].index(o) for o in range(col_count)] for c in range(col_count)],
        np.int32,
    )

    def gather_line(values):
        arrays = [values]
        for kind, source in moves:
            table = (even, odd)[kind]
            arrays.append(lax.ppermute(arrays[source], AXES, pairs(lambda k, c: (k, table[c]))))
        return arrays

    def gather_clus(values):
        parts = {0: values}
        for e in list(range(2, clus_count, 2)) + list(range(1, clus_count, 2)):
            parts[e] = swap(parts[e ^ 1], 1) if e & 1 else swap(values, e)
        return [parts[e] for e in range(clus_count)]

    def per_device(
        density,
        dens_pattern,
        margin_window,
        ovl_pattern,
        keep_mask,
        basis_values,
        rest_density,
        slab_owner,
        cell_lengths,
    ):
        k = lax.axis_index("clus")
        c = lax.axis_index("col")
        rows, cols = dens_pattern.shape
        block = density.shape[0] // rows
        cells = basis_values.shape[2]
        all_blocks = clus_count * rows
        planes, lines, size = rest_density.shape
        devices = clus_count * col_count
        depth = size // devices
        slice_cells = cells // clus_count
        slice_lines = slice_cells // QZ
        patch_lines = cells // QZ
        lines_dev = patch_lines // col_count
        z_start = (size - QZ) // 2
        hartley = cas_table(size)
        hartley_q = jnp.asarray(hartley[z_start : z_start + QZ])
        line_id = np.arange(patch_lines)
        groups = max(1, all_blocks // planes)
        group_size = all_blocks // groups
        y_cells = (
            line_id[None, :] // lines_dev * lines
            + np.arange(groups)[:, None] * lines_dev
            + line_id[None, :] % lines_dev
        )
        hartley_y = jnp.asarray(hartley[y_cells])
        hartley = jnp.asarray(hartley)

        ratio = cols // rows
        device_id = k * col_count + c
        clus_ids = k ^ jnp.arange(clus_count, dtype=jnp.int32)

        own_phi = lax.dynamic_slice_in_dim(basis_values, k * slice_cells, slice_cells, 2)
        pieces = gather_line(own_phi)

        masked = (
            density.reshape(rows, block, cols, block)
            * dens_pattern.astype(jnp.bfloat16)[:, None, :, None]
        ).reshape(rows * block, cols * block)
        gathered = gather_clus(masked)

        rest_lines = rest_density.reshape(planes * lines, size)
        waves = dot_high("kz,lz->kl", hartley, rest_lines)
        moved = exchange((waves * 256.0).astype(jnp.float16).reshape(devices, depth, planes * lines))
        moved = after(moved, pieces[1], pieces[2])
        plane = (
            moved.reshape(clus_count, col_count, depth, planes, lines)
            .transpose(2, 0, 3, 1, 4)
            .reshape(depth, size, size)
            .astype(jnp.float32)
        )
        plane = dot_high("axy,yv->axv", plane, hartley)
        plane = dot_high("ux,axv->auv", hartley * (1.0 / 256.0), plane)

        phi_slice = own_phi.reshape(cols * block, slice_cells)
        margin_masked = (
            margin_window.reshape(cols, block, block)
            * ovl_pattern.astype(jnp.bfloat16)[:, :, None]
        ).reshape(cols * block, block)
        lifted, window = lift(clus_ids, phi_slice, margin_masked, gathered)
        where = jnp.asarray(place)[c][clus_ids // ratio]
        *sent, partial_rho = route(clus_ids, where, clus_ids % ratio, lifted, pieces, rows)
        patch_waves = dot_high(
            "qk,lq->kl", hartley_q, partial_rho.reshape(all_blocks * slice_lines, QZ)
        )
        patch_waves = patch_waves.reshape(devices, depth, all_blocks * slice_lines)
        patch_moved = exchange(patch_waves)
        patch_sum = jnp.sum(
            patch_moved.reshape(
                clus_count, col_count, depth, groups, group_size, slice_lines
            ),
            axis=1,
        )
        patch_sum = patch_sum.transpose(2, 3, 1, 0, 4).reshape(
            groups, group_size, depth, patch_lines
        )
        patch_y = dot_high("gizm,gmv->gizv", patch_sum, hartley_y)
        patch_y = patch_y.reshape(all_blocks, depth, size)
        block_ids = jnp.arange(all_blocks, dtype=jnp.int32)
        x_cells = slab_owner.astype(jnp.int32) * planes + block_ids % planes
        chosen = (x_cells[:, None] == jnp.arange(size, dtype=jnp.int32)[None, :]).astype(jnp.float32)
        hartley_x = jnp.einsum(
            "ix,xu->iu", chosen, hartley, precision=lax.Precision.HIGHEST
        )

        row_parts = []
        for e, part in enumerate(sent):
            row_parts.append(part if e == 0 else swap(part, e))

        plane = plane + dot_high("iu,izv->zuv", hartley_x, patch_y)

        factor = green_planes(cell_lengths, size, device_id * depth, depth) * (1.0 / size**3)
        plane = plane * factor

        picked = dot_high("iu,zuv->izv", hartley_x, plane).reshape(
            groups, group_size, depth, size
        )
        picked = dot_high("gizv,gmv->gizm", picked, hartley_y).reshape(
            clus_count, 1, rows, depth, patch_lines
        )
        picked = jnp.broadcast_to(picked, (clus_count, col_count, rows, depth, patch_lines))
        picked = exchange(picked.reshape(devices, rows, depth, patch_lines))
        patch_pot = dot_high("srdm,sdq->rmq", picked, hartley_q.T.reshape(devices, depth, QZ))
        patch_pot = patch_pot.reshape(rows, cells)

        plane = dot_high("xu,auv->axv", hartley, plane)
        plane = dot_high("axv,vy->axy", plane, hartley)
        back = (
            plane.astype(jnp.bfloat16)
            .reshape(depth, clus_count, planes, col_count, lines)
            .transpose(1, 3, 0, 2, 4)
            .reshape(devices, depth, planes * lines)
        )
        back = exchange(back).reshape(size, planes * lines)
        potential = dot_high("kl,kz->lz", back.astype(jnp.float32), hartley).reshape(
            planes, lines, size
        )

        hartree = hartree_product(
            clus_ids,
            dens_pattern,
            patch_pot,
            basis_values.reshape(cols * block, cells),
            row_parts,
        )

        span = clus_count // col_count
        window = (window * 32.0).astype(jnp.float16)
        window = lax.all_to_all(window, "clus", split_axis=0, concat_axis=0, tiled=True)
        window = window.reshape(col_count, span, block, block)
        summed = 0.0
        for step in range(col_count):
            part = lax.dynamic_index_in_dim(window, c ^ step, 0, keepdims=False)
            if step:
                part = lax.ppermute(part, AXES, pairs(lambda k, c: (k, c ^ step)))
            summed = summed + part.astype(jnp.float32)
        summed = summed * (keep_mask.astype(jnp.float32)[0][:, None, None] * (1.0 / 32.0))
        product = summed.transpose(1, 0, 2).reshape(block, span * block).astype(jnp.bfloat16)
        return (potential, hartree, product)

    return per_device


def solution(mesh):
    in_specs = (
        P("clus", "col"),
        P("clus", "col"),
        P("col", "clus"),
        P("col", "clus"),
        P("clus", "col"),
        P("col", None, None),
        P("clus", "col", None),
        P(),
        P(),
    )
    out_specs = (P("clus", "col", None), P("clus", "col"), P("clus", "col"))
    clus_count, col_count = mesh.shape["clus"], mesh.shape["col"]
    return jax.shard_map(
        make_program(clus_count, col_count),
        mesh=mesh,
        in_specs=in_specs,
        out_specs=out_specs,
        check_vma=False,
    )
```

```python
import math

import jax
import jax.numpy as jnp
import numpy as np
from jax import lax
from jax.experimental import pallas as pl
from jax.experimental.pallas import tpu as pltpu
from jax.sharding import PartitionSpec as P


QZ = 128
AXES = ("clus", "col")
HIGH = lax.Precision.HIGH


def cas_table(size):
    counter = np.arange(size)
    angles = (counter[:, None] * counter[None, :] % size) * (2.0 * math.pi / size)
    return (np.cos(angles) + np.sin(angles)).astype(np.float32)


def dot_high(equation, left_side, right_side):
    return jnp.einsum(
        equation, left_side, right_side, precision=HIGH, preferred_element_type=jnp.float32
    )


def exchange(values):
    return lax.all_to_all(values, AXES, split_axis=0, concat_axis=0, tiled=True)


def green_planes(cell_lengths, size, first, depth):
    def squared_wave(frequency, axis_pos):
        signed = jnp.where(frequency < size // 2, frequency, frequency - size).astype(jnp.float32)
        scaled = signed * (2.0 * math.pi) / cell_lengths[axis_pos]
        return scaled * scaled

    freq_z = first + jnp.arange(depth, dtype=jnp.int32)[:, None, None]
    freq_x = jnp.arange(size, dtype=jnp.int32)[None, :, None]
    freq_y = jnp.arange(size, dtype=jnp.int32)[None, None, :]
    squared = squared_wave(freq_x, 0) + squared_wave(freq_y, 1) + squared_wave(freq_z, 2)
    at_anchor = (freq_x == 0) & (freq_y == 0) & (freq_z == 0)
    return jnp.where(at_anchor, 0.0, 4.0 * math.pi / jnp.where(at_anchor, 1.0, squared))


def after(values, *others):
    return lax.optimization_barrier((values,) + others)[0]


def lift_kernel(order_ref, basis_ref, margin_ref, *refs, places, held_before):
    part_refs = refs[: len(places)]
    lifted_ref, window_ref, held = refs[len(places) + held_before :]
    step = pl.program_id(0)
    for part_ref, (e, start) in zip(part_refs, places):

        @pl.when(step == e)
        def _(part_ref=part_ref, start=start):
            held[start : start + part_ref.shape[0], :] = part_ref[...]

    block = margin_ref.shape[1]
    window_ref[0] = jnp.dot(
        held[:block, :], margin_ref[...], preferred_element_type=jnp.float32
    )

    @pl.loop(0, held.shape[0] // block)
    def _(i):
        at = pl.ds(pl.multiple_of(i * block, block), block)
        lifted_ref[0, at, :] = jnp.dot(
            held[at, :], basis_ref[...], preferred_element_type=jnp.float32
        )


def lift(order, basis, margin, parts, total, before=()):
    count = order.shape[0]
    pieces = [piece for part in parts for piece in part]
    places = []
    for e, part in enumerate(parts):
        start = 0
        for piece in part:
            places.append((e, start))
            start += piece.shape[0]
    height, depth = start, pieces[0].shape[1]
    width, block = basis.shape[1], margin.shape[1]
    once = pl.Buffered(1)
    whole = lambda i, s: (0, 0)
    first_before = 3 + len(pieces)
    return pl.pallas_call(
        lambda *refs: lift_kernel(*refs, places=places, held_before=len(before)),
        out_shape=[
            jax.ShapeDtypeStruct((total, height, width), jnp.float32),
            jax.ShapeDtypeStruct((total, block, block), jnp.float32),
        ],
        grid_spec=pltpu.PrefetchScalarGridSpec(
            num_scalar_prefetch=1,
            grid=(count,),
            in_specs=[
                pl.BlockSpec((depth, width), whole, pipeline_mode=once),
                pl.BlockSpec((depth, block), whole, pipeline_mode=once),
            ]
            + [pl.BlockSpec(piece.shape, whole, pipeline_mode=once) for piece in pieces]
            + [pl.BlockSpec(memory_space=pl.ANY) for _ in before],
            out_specs=[
                pl.BlockSpec((1, height, width), lambda i, s: (s[i], 0, 0)),
                pl.BlockSpec((1, block, block), lambda i, s: (s[i], 0, 0)),
            ],
            scratch_shapes=[pltpu.VMEM((height, depth), jnp.bfloat16)],
        ),
        input_output_aliases={first_before + i: i for i in range(len(before))},
        cost_estimate=pl.CostEstimate(
            flops=2 * height * depth * width * count,
            bytes_accessed=count * (2 * height * depth + 4 * height * width),
            transcendentals=0,
        ),
        name="lift",
    )(order, basis, margin, *pieces, *before)


def route_kernel(owner_ref, where_ref, part_ref, lifted_ref, *refs, pieces, outs):
    piece_refs, out_refs = refs[:pieces], refs[pieces : pieces + outs]
    rho_ref, held, in_sems, out_sems = refs[pieces + outs :]
    rows = held.shape[1]
    step = pl.program_id(0)

    @pl.when(step == 0)
    def _():
        for e in range(outs):
            start = part_ref[e] * rows
            for p in range(pieces):

                @pl.when(where_ref[e] == p)
                def _(e=e, p=p, start=start):
                    pltpu.make_async_copy(
                        piece_refs[p].at[pl.ds(start, rows)], held.at[e], in_sems.at[e]
                    ).start()

    pltpu.make_async_copy(
        piece_refs[0].at[pl.ds(0, rows)], held.at[step], in_sems.at[step]
    ).wait()
    for e in range(outs):

        @pl.when(step == e)
        def _(e=e):
            pltpu.make_async_copy(held.at[e], out_refs[e], out_sems.at[e]).start()

    for b in range(rows):
        basis = held[step, b].astype(jnp.float32)
        height = basis.shape[0]
        rho_ref[0, b : b + 1, :] = jnp.sum(
            basis * lifted_ref[0, b * height : (b + 1) * height, :], axis=0, keepdims=True
        )

    @pl.when(step == outs - 1)
    def _():
        for e in range(outs):
            pltpu.make_async_copy(held.at[e], out_refs[e], out_sems.at[e]).wait()


def route(owner, where, part, lifted, pieces, rows):
    outs = where.shape[0]
    shape = (rows,) + pieces[0].shape[1:]
    height, width = lifted.shape[1:]
    size = math.prod(shape) * outs
    return pl.pallas_call(
        lambda *refs: route_kernel(*refs, pieces=len(pieces), outs=outs),
        out_shape=[jax.ShapeDtypeStruct(shape, pieces[0].dtype)] * outs
        + [jax.ShapeDtypeStruct((outs, rows, width), jnp.float32)],
        grid_spec=pltpu.PrefetchScalarGridSpec(
            num_scalar_prefetch=3,
            grid=(outs,),
            in_specs=[pl.BlockSpec((1, height, width), lambda i, o, w, p: (o[i], 0, 0))]
            + [pl.BlockSpec(memory_space=pl.ANY)] * len(pieces),
            out_specs=[pl.BlockSpec(memory_space=pl.ANY)] * outs
            + [pl.BlockSpec((1, rows, width), lambda i, o, w, p: (o[i], 0, 0))],
            scratch_shapes=[
                pltpu.VMEM((outs,) + shape, pieces[0].dtype),
                pltpu.SemaphoreType.DMA((outs,)),
                pltpu.SemaphoreType.DMA((outs,)),
            ],
        ),
        cost_estimate=pl.CostEstimate(
            flops=2 * size, bytes_accessed=4 * size + 4 * size, transcendentals=0
        ),
        name="route",
    )(owner, where, part, lifted, *pieces)


def hartree_kernel(slot_ref, pattern_ref, pot_ref, columns_ref, *refs, count):
    row_refs, out_ref, scaled = refs[:count], refs[count], refs[count + 1]
    step = pl.program_id(0)
    rows, block, width = row_refs[0].shape

    @pl.when(step == 0)
    def _():
        for e in range(count):
            at = pl.ds(pl.multiple_of(slot_ref[e] * width, width), width)
            for b in range(rows):
                scaled[pl.ds(b * block, block), at] = (
                    row_refs[e][b].astype(jnp.float32) * pot_ref[b : b + 1, at]
                ).astype(jnp.bfloat16)

    @pl.loop(0, rows)
    def _(b):
        at = pl.ds(pl.multiple_of(b * block, block), block)
        keep = pattern_ref[b, step].astype(jnp.float32)
        values = lax.dot_general(
            scaled[at, :],
            columns_ref[...],
            (((1,), (1,)), ((), ())),
            preferred_element_type=jnp.float32,
        )
        out_ref[at, :] = (values * keep).astype(jnp.bfloat16)


def hartree_product(slots, pattern, pot, columns, row_parts):
    count = len(row_parts)
    rows, block, width = row_parts[0].shape
    depth, cells = columns.shape
    height = rows * block
    once = pl.Buffered(1)
    return pl.pallas_call(
        lambda *refs: hartree_kernel(*refs, count=count),
        out_shape=jax.ShapeDtypeStruct((height, depth), jnp.bfloat16),
        grid_spec=pltpu.PrefetchScalarGridSpec(
            num_scalar_prefetch=2,
            grid=(depth // block,),
            in_specs=[
                pl.BlockSpec(pot.shape, lambda i, s, p: (0, 0), pipeline_mode=once),
                pl.BlockSpec((block, cells), lambda i, s, p: (i, 0)),
            ]
            + [
                pl.BlockSpec((rows, block, width), lambda i, s, p: (0, 0, 0), pipeline_mode=once)
                for _ in row_parts
            ],
            out_specs=pl.BlockSpec((height, block), lambda i, s, p: (0, i)),
            scratch_shapes=[pltpu.VMEM((height, cells), jnp.bfloat16)],
        ),
        cost_estimate=pl.CostEstimate(
            flops=2 * height * depth * cells,
            bytes_accessed=2 * (depth + height) * cells,
            transcendentals=0,
        ),
        name="hartree",
    )(slots, pattern, pot, columns, *row_parts)


def make_program(clus_count, col_count):
    def pairs(move):
        return [
            (k * col_count + c, k2 * col_count + c2)
            for k in range(clus_count)
            for c in range(col_count)
            for k2, c2 in [move(k, c)]
            if 0 <= c2 < col_count
        ]

    def swap(values, distance):
        return lax.ppermute(values, AXES, pairs(lambda k, c: (k ^ distance, c)))

    even = [c ^ 1 for c in range(col_count)]
    odd = [c if c in (0, col_count - 1) else c - 1 if c % 2 == 0 else c + 1 for c in range(col_count)]
    moves = []
    holds = [list(range(col_count))]
    tips = [0, 0]
    while any(len({h[c] for h in holds} - {-1}) < col_count for c in range(col_count)):
        made = []
        for kind, table in enumerate((even, odd)):
            if tips[kind] is None:
                made.append(None)
                continue
            source = holds[tips[kind]]
            arrived = [-1 if table[c] == c else source[table[c]] for c in range(col_count)]
            if all(arrived[c] in [-1] + [h[c] for h in holds] for c in range(col_count)):
                made.append(None)
                continue
            moves.append((kind, tips[kind]))
            holds.append(arrived)
            made.append(len(holds) - 1)
        tips = [made[1], made[0]]
    place = np.array(
        [[[h[c] for h in holds].index(o) for o in range(col_count)] for c in range(col_count)],
        np.int32,
    )

    def gather_line(values):
        arrays = [values]
        for kind, source in moves:
            table = (even, odd)[kind]
            moved = pairs(lambda k, c: (k, table[c]) if table[c] != c else (k ^ 1, c))
            arrays.append(lax.ppermute(arrays[source], AXES, moved))
        return arrays

    def gather_clus(values):
        half = values.shape[0] // 2
        parts = {0: [values]}
        evens = sorted(range(2, clus_count, 2), key=lambda e: bin(e).count("1"))
        for e in evens + list(range(1, clus_count, 2)):
            bits = [1 << b for b in range(clus_count.bit_length()) if e >> b & 1]
            if e & 1:
                parts[e] = [swap(piece, 1) for piece in parts[e ^ 1]]
            elif len(bits) == 2:
                first, second = parts[bits[0]][0], parts[bits[1]][0]
                parts[e] = [swap(first[:half], bits[1]), swap(second[half:], bits[0])]
            else:
                parts[e] = [swap(values, e)]
        return [parts[e] for e in range(clus_count)]

    def per_device(
        density,
        dens_pattern,
        margin_window,
        ovl_pattern,
        keep_mask,
        basis_values,
        rest_density,
        slab_owner,
        cell_lengths,
    ):
        k = lax.axis_index("clus")
        c = lax.axis_index("col")
        rows, cols = dens_pattern.shape
        block = density.shape[0] // rows
        cells = basis_values.shape[2]
        all_blocks = clus_count * rows
        planes, lines, size = rest_density.shape
        devices = clus_count * col_count
        depth = size // devices
        slice_cells = cells // clus_count
        slice_lines = slice_cells // QZ
        patch_lines = cells // QZ
        lines_dev = patch_lines // col_count
        z_start = (size - QZ) // 2
        hartley = cas_table(size)
        hartley_q = jnp.asarray(hartley[z_start : z_start + QZ])
        line_id = np.arange(patch_lines)
        groups = max(1, all_blocks // planes)
        group_size = all_blocks // groups
        y_cells = (
            line_id[None, :] // lines_dev * lines
            + np.arange(groups)[:, None] * lines_dev
            + line_id[None, :] % lines_dev
        )
        hartley_y = jnp.asarray(hartley[y_cells])
        hartley = jnp.asarray(hartley)

        ratio = cols // rows
        device_id = k * col_count + c
        clus_ids = k ^ jnp.arange(clus_count, dtype=jnp.int32)

        own_phi = lax.dynamic_slice_in_dim(basis_values, k * slice_cells, slice_cells, 2)
        pieces = gather_line(own_phi)

        masked = (
            density.reshape(rows, block, cols, block)
            * dens_pattern.astype(jnp.bfloat16)[:, None, :, None]
        ).reshape(rows * block, cols * block)
        gathered = gather_clus(masked)

        rest_lines = rest_density.reshape(planes * lines, size)
        waves = dot_high("kz,lz->kl", hartley, rest_lines)
        moved = exchange((waves * 256.0).astype(jnp.float16).reshape(devices, depth, planes * lines))
        moved = after(moved, pieces[1], pieces[2])
        plane = (
            moved.reshape(clus_count, col_count, depth, planes, lines)
            .transpose(2, 0, 3, 1, 4)
            .reshape(depth, size, size)
            .astype(jnp.float32)
        )
        plane = dot_high("axy,yv->axv", plane, hartley)
        plane = dot_high("ux,axv->auv", hartley * (1.0 / 256.0), plane)

        phi_slice = own_phi.reshape(cols * block, slice_cells)
        margin_masked = (
            margin_window.reshape(cols, block, block)
            * ovl_pattern.astype(jnp.bfloat16)[:, :, None]
        ).reshape(cols * block, block)
        split = clus_count // 2
        before = lift(
            clus_ids[:split], phi_slice, margin_masked, gathered[:split], clus_count
        )
        lifted, window = lift(
            clus_ids[split:], phi_slice, margin_masked, gathered[split:], clus_count, before
        )
        where = jnp.asarray(place)[c][clus_ids // ratio]
        *sent, partial_rho = route(clus_ids, where, clus_ids % ratio, lifted, pieces, rows)
        patch_waves = dot_high(
            "qk,lq->kl", hartley_q, partial_rho.reshape(all_blocks * slice_lines, QZ)
        )
        patch_waves = patch_waves.reshape(devices, depth, all_blocks * slice_lines)
        patch_moved = exchange(patch_waves)
        patch_sum = jnp.sum(
            patch_moved.reshape(
                clus_count, col_count, depth, groups, group_size, slice_lines
            ),
            axis=1,
        )
        patch_sum = patch_sum.transpose(2, 3, 1, 0, 4).reshape(
            groups, group_size, depth, patch_lines
        )
        patch_y = dot_high("gizm,gmv->gizv", patch_sum, hartley_y)
        patch_y = patch_y.reshape(all_blocks, depth, size)
        block_ids = jnp.arange(all_blocks, dtype=jnp.int32)
        x_cells = slab_owner.astype(jnp.int32) * planes + block_ids % planes
        chosen = (x_cells[:, None] == jnp.arange(size, dtype=jnp.int32)[None, :]).astype(jnp.float32)
        hartley_x = jnp.einsum(
            "ix,xu->iu", chosen, hartley, precision=lax.Precision.HIGHEST
        )

        row_parts = []
        for e, part in enumerate(sent):
            row_parts.append(part if e == 0 else swap(part, e))

        plane = plane + dot_high("iu,izv->zuv", hartley_x, patch_y)

        factor = green_planes(cell_lengths, size, device_id * depth, depth) * (1.0 / size**3)
        plane = plane * factor

        picked = dot_high("iu,zuv->izv", hartley_x, plane).reshape(
            groups, group_size, depth, size
        )
        picked = dot_high("gizv,gmv->gizm", picked, hartley_y).reshape(
            clus_count, rows, depth, patch_lines
        )
        picked = picked.transpose(0, 2, 1, 3).reshape(clus_count, 1, depth, rows * patch_lines)
        leading = lax.reduce_precision(picked, 8, 7)
        picked = jnp.concatenate([leading, picked - leading], axis=-1).astype(jnp.bfloat16)
        picked = jnp.broadcast_to(
            picked, (clus_count, col_count, depth, 2 * rows * patch_lines)
        ).reshape(devices, depth, 2 * rows * patch_lines)

        plane = dot_high("xu,auv->axv", hartley, plane)
        plane = dot_high("axv,vy->axy", plane, hartley)
        back = (
            plane.astype(jnp.bfloat16)
            .reshape(depth, clus_count, planes, col_count, lines)
            .transpose(1, 3, 0, 2, 4)
            .reshape(devices, depth, planes * lines)
        )
        back = jnp.concatenate([back, picked], axis=-1)
        back = exchange(back).reshape(size, planes * lines + 2 * rows * patch_lines)
        picked = back[:, planes * lines :].astype(jnp.float32).reshape(size, 2, rows, patch_lines)
        patch_pot = dot_high("krm,qk->rmq", picked[:, 0] + picked[:, 1], hartley_q)
        patch_pot = patch_pot.reshape(rows, cells)
        back = back[:, : planes * lines].astype(jnp.float32)
        potential = dot_high("kl,kz->lz", back, hartley).reshape(planes, lines, size)

        hartree = hartree_product(
            clus_ids,
            dens_pattern,
            patch_pot,
            basis_values.reshape(cols * block, cells),
            row_parts,
        )

        span = clus_count // col_count
        window = (window * 32.0).astype(jnp.float16)
        window = lax.all_to_all(window, "clus", split_axis=0, concat_axis=0, tiled=True)
        window = window.reshape(col_count, span, block, block)
        summed = 0.0
        for step in range(col_count):
            part = lax.dynamic_index_in_dim(window, c ^ step, 0, keepdims=False)
            if step:
                part = lax.ppermute(part, AXES, pairs(lambda k, c: (k, c ^ step)))
            summed = summed + part.astype(jnp.float32)
        summed = summed * (keep_mask.astype(jnp.float32)[0][:, None, None] * (1.0 / 32.0))
        product = summed.transpose(1, 0, 2).reshape(block, span * block).astype(jnp.bfloat16)
        return (potential, hartree, product)

    return per_device


def solution(mesh):
    in_specs = (
        P("clus", "col"),
        P("clus", "col"),
        P("col", "clus"),
        P("col", "clus"),
        P("clus", "col"),
        P("col", None, None),
        P("clus", "col", None),
        P(),
        P(),
    )
    out_specs = (P("clus", "col", None), P("clus", "col"), P("clus", "col"))
    clus_count, col_count = mesh.shape["clus"], mesh.shape["col"]
    return jax.shard_map(
        make_program(clus_count, col_count),
        mesh=mesh,
        in_specs=in_specs,
        out_specs=out_specs,
        check_vma=False,
    )
```

```python
import math

import jax
import jax.numpy as jnp
import numpy as np
from jax import lax
from jax.experimental import pallas as pl
from jax.experimental.pallas import tpu as pltpu
from jax.sharding import PartitionSpec as P


QZ = 128
AXES = ("clus", "col")
HIGH = lax.Precision.HIGH


def cas_table(size):
    counter = np.arange(size)
    angles = (counter[:, None] * counter[None, :] % size) * (2.0 * math.pi / size)
    return (np.cos(angles) + np.sin(angles)).astype(np.float32)


def dot_high(equation, left_side, right_side):
    return jnp.einsum(
        equation, left_side, right_side, precision=HIGH, preferred_element_type=jnp.float32
    )


def exchange(values):
    return lax.all_to_all(values, AXES, split_axis=0, concat_axis=0, tiled=True)


def green_planes(cell_lengths, size, first, depth):
    def squared_wave(frequency, axis_pos):
        signed = jnp.where(frequency < size // 2, frequency, frequency - size).astype(jnp.float32)
        scaled = signed * (2.0 * math.pi) / cell_lengths[axis_pos]
        return scaled * scaled

    freq_z = first + jnp.arange(depth, dtype=jnp.int32)[:, None, None]
    freq_x = jnp.arange(size, dtype=jnp.int32)[None, :, None]
    freq_y = jnp.arange(size, dtype=jnp.int32)[None, None, :]
    squared = squared_wave(freq_x, 0) + squared_wave(freq_y, 1) + squared_wave(freq_z, 2)
    at_anchor = (freq_x == 0) & (freq_y == 0) & (freq_z == 0)
    return jnp.where(at_anchor, 0.0, 4.0 * math.pi / jnp.where(at_anchor, 1.0, squared))


def lift_kernel(order_ref, basis_ref, margin_ref, *refs, places, held_before):
    part_refs = refs[: len(places)]
    lifted_ref, window_ref, held, sems = refs[len(places) + held_before :]
    step = pl.program_id(0)

    def copies(e):
        return [
            pltpu.make_async_copy(
                part_ref, held.at[e, pl.ds(start, part_ref.shape[0])], sems.at[i]
            )
            for i, (part_ref, (owner, start)) in enumerate(zip(part_refs, places))
            if owner == e
        ]

    @pl.when(step == 0)
    def _():
        for e in range(held.shape[0]):
            for copy in copies(e):
                copy.start()

    for e in range(held.shape[0]):

        @pl.when(step == e)
        def _(e=e):
            for copy in copies(e):
                copy.wait()

    block = margin_ref.shape[1]
    window_ref[0] = jnp.dot(
        held[step, :block, :], margin_ref[...], preferred_element_type=jnp.float32
    )

    @pl.loop(0, held.shape[1] // block)
    def _(i):
        at = pl.ds(pl.multiple_of(i * block, block), block)
        lifted_ref[0, at, :] = jnp.dot(
            held[step, at, :], basis_ref[...], preferred_element_type=jnp.float32
        )


def lift(order, basis, margin, parts, total, first, before=()):
    count = order.shape[0]
    pieces = [piece for part in parts for piece in part]
    places = []
    for e, part in enumerate(parts):
        start = 0
        for piece in part:
            places.append((e, start))
            start += piece.shape[0]
    height, depth = start, pieces[0].shape[1]
    width, block = basis.shape[1], margin.shape[1]
    once = pl.Buffered(1)
    whole = lambda i, s: (0, 0)
    first_before = 3 + len(pieces)
    return pl.pallas_call(
        lambda *refs: lift_kernel(*refs, places=places, held_before=len(before)),
        out_shape=[
            jax.ShapeDtypeStruct((total, height, width), jnp.float32),
            jax.ShapeDtypeStruct((total, block, block), jnp.float32),
        ],
        grid_spec=pltpu.PrefetchScalarGridSpec(
            num_scalar_prefetch=1,
            grid=(count,),
            in_specs=[
                pl.BlockSpec((depth, width), whole, pipeline_mode=once),
                pl.BlockSpec((depth, block), whole, pipeline_mode=once),
            ]
            + [pl.BlockSpec(memory_space=pl.ANY) for _ in pieces + list(before)],
            out_specs=[
                pl.BlockSpec((1, height, width), lambda i, s: (s[i], 0, 0)),
                pl.BlockSpec((1, block, block), lambda i, s: (first + i, 0, 0)),
            ],
            scratch_shapes=[
                pltpu.VMEM((count, height, depth), jnp.bfloat16),
                pltpu.SemaphoreType.DMA((len(pieces),)),
            ],
        ),
        input_output_aliases={first_before + i: i for i in range(len(before))},
        cost_estimate=pl.CostEstimate(
            flops=2 * height * depth * width * count,
            bytes_accessed=count * (2 * height * depth + 4 * height * width),
            transcendentals=0,
        ),
        name="lift",
    )(order, basis, margin, *pieces, *before)


def route_kernel(owner_ref, where_ref, part_ref, lifted_ref, *refs, pieces, outs):
    piece_refs, out_refs = refs[:pieces], refs[pieces : pieces + outs]
    rho_ref, held, in_sems, out_sems = refs[pieces + outs :]
    rows = held.shape[1]
    step = pl.program_id(0)

    @pl.when(step == 0)
    def _():
        for e in range(outs):
            start = part_ref[e] * rows
            for p in range(pieces):

                @pl.when(where_ref[e] == p)
                def _(e=e, p=p, start=start):
                    pltpu.make_async_copy(
                        piece_refs[p].at[pl.ds(start, rows)], held.at[e], in_sems.at[e]
                    ).start()

    pltpu.make_async_copy(
        piece_refs[0].at[pl.ds(0, rows)], held.at[step], in_sems.at[step]
    ).wait()
    for e in range(outs):

        @pl.when(step == e)
        def _(e=e):
            pltpu.make_async_copy(held.at[e], out_refs[e], out_sems.at[e]).start()

    for b in range(rows):
        basis = held[step, b].astype(jnp.float32)
        height = basis.shape[0]
        rho_ref[0, b : b + 1, :] = jnp.sum(
            basis * lifted_ref[0, b * height : (b + 1) * height, :], axis=0, keepdims=True
        )

    @pl.when(step == outs - 1)
    def _():
        for e in range(outs):
            pltpu.make_async_copy(held.at[e], out_refs[e], out_sems.at[e]).wait()


def route(owner, where, part, lifted, pieces, rows):
    outs = where.shape[0]
    shape = (rows,) + pieces[0].shape[1:]
    height, width = lifted.shape[1:]
    size = math.prod(shape) * outs
    return pl.pallas_call(
        lambda *refs: route_kernel(*refs, pieces=len(pieces), outs=outs),
        out_shape=[jax.ShapeDtypeStruct(shape, pieces[0].dtype)] * outs
        + [jax.ShapeDtypeStruct((outs, rows, width), jnp.float32)],
        grid_spec=pltpu.PrefetchScalarGridSpec(
            num_scalar_prefetch=3,
            grid=(outs,),
            in_specs=[pl.BlockSpec((1, height, width), lambda i, o, w, p: (o[i], 0, 0))]
            + [pl.BlockSpec(memory_space=pl.ANY)] * len(pieces),
            out_specs=[pl.BlockSpec(memory_space=pl.ANY)] * outs
            + [pl.BlockSpec((1, rows, width), lambda i, o, w, p: (o[i], 0, 0))],
            scratch_shapes=[
                pltpu.VMEM((outs,) + shape, pieces[0].dtype),
                pltpu.SemaphoreType.DMA((outs,)),
                pltpu.SemaphoreType.DMA((outs,)),
            ],
        ),
        cost_estimate=pl.CostEstimate(
            flops=2 * size, bytes_accessed=4 * size + 4 * size, transcendentals=0
        ),
        name="route",
    )(owner, where, part, lifted, *pieces)


def hartree_kernel(slot_ref, pattern_ref, pot_ref, columns_ref, *refs, count):
    row_refs, out_ref, scaled = refs[:count], refs[count], refs[count + 1]
    step = pl.program_id(0)
    rows, block, width = row_refs[0].shape

    @pl.when(step == 0)
    def _():
        for e in range(count):
            at = pl.ds(pl.multiple_of(slot_ref[e] * width, width), width)
            for b in range(rows):
                scaled[pl.ds(b * block, block), at] = (
                    row_refs[e][b].astype(jnp.float32) * pot_ref[b : b + 1, at]
                ).astype(jnp.bfloat16)

    @pl.loop(0, rows)
    def _(b):
        at = pl.ds(pl.multiple_of(b * block, block), block)
        keep = pattern_ref[b, step].astype(jnp.float32)
        values = lax.dot_general(
            scaled[at, :],
            columns_ref[...],
            (((1,), (1,)), ((), ())),
            preferred_element_type=jnp.float32,
        )
        out_ref[at, :] = (values * keep).astype(jnp.bfloat16)


def hartree_product(slots, pattern, pot, columns, row_parts):
    count = len(row_parts)
    rows, block, width = row_parts[0].shape
    depth, cells = columns.shape
    height = rows * block
    once = pl.Buffered(1)
    return pl.pallas_call(
        lambda *refs: hartree_kernel(*refs, count=count),
        out_shape=jax.ShapeDtypeStruct((height, depth), jnp.bfloat16),
        grid_spec=pltpu.PrefetchScalarGridSpec(
            num_scalar_prefetch=2,
            grid=(depth // block,),
            in_specs=[
                pl.BlockSpec(pot.shape, lambda i, s, p: (0, 0), pipeline_mode=once),
                pl.BlockSpec((block, cells), lambda i, s, p: (i, 0)),
            ]
            + [
                pl.BlockSpec((rows, block, width), lambda i, s, p: (0, 0, 0), pipeline_mode=once)
                for _ in row_parts
            ],
            out_specs=pl.BlockSpec((height, block), lambda i, s, p: (0, i)),
            scratch_shapes=[pltpu.VMEM((height, cells), jnp.bfloat16)],
        ),
        cost_estimate=pl.CostEstimate(
            flops=2 * height * depth * cells,
            bytes_accessed=2 * (depth + height) * cells,
            transcendentals=0,
        ),
        name="hartree",
    )(slots, pattern, pot, columns, *row_parts)


def split_table(table):
    leading = table.astype(jnp.bfloat16)
    return leading, (table - leading.astype(np.float32)).astype(jnp.bfloat16)


def split_values(values):
    leading = values.astype(jnp.bfloat16)
    return leading, (values - leading.astype(jnp.float32)).astype(jnp.bfloat16)


def dot_split(left_side, right_side):
    dot = lambda a, b: jnp.dot(a, b, preferred_element_type=jnp.float32)
    return (
        dot(left_side[0], right_side[0])
        + dot(left_side[0], right_side[1])
        + dot(left_side[1], right_side[0])
    )


def merge_lanes(part_of, count, width, shift_of):
    lane = lax.broadcasted_iota(jnp.int32, (1, 128), 1)
    merged = None
    for i in range(count):
        shift = shift_of(i) * width % 128
        part = part_of(i)
        part = pltpu.roll(part, shift, 1) if shift else part
        merged = part if merged is None else jnp.where(lane >= i * width, part, merged)
    return merged


def forward_kernel(values_ref, xh_ref, xl_ref, yh_ref, yl_ref, out_ref, *, clus, col, lines):
    size = out_ref.shape[1]
    fold = 128 // lines

    def source(c):
        return jnp.concatenate([values_ref[k * col + c, 0] for k in range(clus)], axis=0)

    sources = [source(c) for c in range(col)]
    plane = jnp.concatenate(
        [
            jnp.concatenate(
                [
                    merge_lanes(lambda s: sources[j * fold + s], fold, lines, lambda s: s - p)
                    for j in range(size // 128)
                ],
                axis=1,
            )
            for p in range(fold)
        ],
        axis=0,
    )
    plane = dot_split(split_values(plane), (yh_ref[...], yl_ref[...]))
    out_ref[0] = dot_split((xh_ref[...], xl_ref[...]), split_values(plane))


def forward_planes(values, x_table, y_table, clus, col, lines):
    devices, depth, tiles, lanes = values.shape
    size = x_table[0].shape[0]
    table = pl.BlockSpec((size, size), lambda i: (0, 0), pipeline_mode=pl.Buffered(1))
    return pl.pallas_call(
        lambda *refs: forward_kernel(*refs, clus=clus, col=col, lines=lines),
        out_shape=jax.ShapeDtypeStruct((depth, size, size), jnp.float32),
        grid=(depth,),
        in_specs=[pl.BlockSpec((devices, 1, tiles, lanes), lambda i: (0, i, 0, 0))] + [table] * 4,
        out_specs=pl.BlockSpec((1, size, size), lambda i: (i, 0, 0)),
        cost_estimate=pl.CostEstimate(
            flops=12 * depth * size**3, bytes_accessed=8 * depth * size**2, transcendentals=0
        ),
        name="forward",
    )(values, *x_table, *y_table)


def inverse_kernel(
    plane_ref, factor_ref, patch_ref, spread_ref, pick_ref, lines_ref, *refs, clus, col, lines
):
    xh_ref, xl_ref, yh_ref, yl_ref, out_ref, held = refs
    step = pl.program_id(0)
    depth, tiles = held.shape[0], out_ref.shape[2]
    fold = 128 // lines
    exact = lambda a, b: jnp.dot(
        a, b, precision=lax.Precision.HIGHEST, preferred_element_type=jnp.float32
    )
    plane = (plane_ref[0] + exact(spread_ref[...], patch_ref[0])) * factor_ref[0]
    picked = None
    for b in range(pick_ref.shape[0]):
        value = exact(exact(pick_ref[b], plane), lines_ref[b])
        picked = value if picked is None else picked + value
    lane = lax.broadcasted_iota(jnp.int32, picked.shape, 1)
    leading = picked.astype(jnp.bfloat16).astype(jnp.float32)
    held[step] = jnp.where(lane < 64, picked, picked - leading)
    plane = dot_split((xh_ref[...], xl_ref[...]), split_values(plane))
    plane = dot_split(split_values(plane), (yh_ref[...], yl_ref[...]))
    height = clus * tiles
    for c in range(col):
        at = c // fold * 128
        merged = merge_lanes(
            lambda p: plane[p * height : (p + 1) * height, at : at + 128],
            fold,
            lines,
            lambda p: p - c % fold,
        ).astype(jnp.bfloat16)
        for k in range(clus):
            out_ref[k * col + c, step] = merged[k * tiles : (k + 1) * tiles]

    @pl.when(step == depth - 1)
    def _():
        for k in range(clus):
            rows = jnp.concatenate(
                [held[:, k, :], jnp.zeros((tiles - depth, 128), jnp.float32)], axis=0
            ).astype(jnp.bfloat16)
            for c in range(col):
                out_ref[k * col + c, depth] = rows


def inverse_planes(plane, factor, patch, spread, pick, line_table, x_table, y_table, tiles, clus, col, lines):
    depth, size, _ = plane.shape
    blocks = patch.shape[1]
    devices = clus * col
    once = pl.Buffered(1)
    whole = lambda array: pl.BlockSpec(
        array.shape, lambda i: (0,) * array.ndim, pipeline_mode=once
    )
    by_plane = pl.BlockSpec((1, size, size), lambda i: (i, 0, 0))
    constants = (spread, pick, line_table, *x_table, *y_table)
    return pl.pallas_call(
        lambda *refs: inverse_kernel(*refs, clus=clus, col=col, lines=lines),
        out_shape=jax.ShapeDtypeStruct((devices, depth + 1, tiles, 128), jnp.bfloat16),
        grid=(depth,),
        in_specs=[by_plane, by_plane, pl.BlockSpec((1, blocks, size), lambda i: (i, 0, 0))]
        + [whole(array) for array in constants],
        out_specs=pl.BlockSpec((devices, depth + 1, tiles, 128), lambda i: (0, 0, 0, 0)),
        scratch_shapes=[pltpu.VMEM((depth, clus, 128), jnp.float32)],
        cost_estimate=pl.CostEstimate(
            flops=12 * depth * size**3, bytes_accessed=10 * depth * size**2, transcendentals=0
        ),
        name="inverse",
    )(plane, factor, patch, *constants)


def make_program(clus_count, col_count):
    def pairs(move):
        return [
            (k * col_count + c, k2 * col_count + c2)
            for k in range(clus_count)
            for c in range(col_count)
            for k2, c2 in [move(k, c)]
            if 0 <= c2 < col_count
        ]

    def swap(values, distance):
        return lax.ppermute(values, AXES, pairs(lambda k, c: (k ^ distance, c)))

    even = [c ^ 1 for c in range(col_count)]
    odd = [c if c in (0, col_count - 1) else c - 1 if c % 2 == 0 else c + 1 for c in range(col_count)]
    moves = []
    holds = [list(range(col_count))]
    tips = [0, 0]
    while any(len({h[c] for h in holds} - {-1}) < col_count for c in range(col_count)):
        made = []
        for kind, table in enumerate((even, odd)):
            if tips[kind] is None:
                made.append(None)
                continue
            source = holds[tips[kind]]
            arrived = [-1 if table[c] == c else source[table[c]] for c in range(col_count)]
            if all(arrived[c] in [-1] + [h[c] for h in holds] for c in range(col_count)):
                made.append(None)
                continue
            moves.append((kind, tips[kind]))
            holds.append(arrived)
            made.append(len(holds) - 1)
        tips = [made[1], made[0]]
    place = np.array(
        [[[h[c] for h in holds].index(o) for o in range(col_count)] for c in range(col_count)],
        np.int32,
    )

    def gather_line(values):
        arrays = [values]
        for kind, source in moves:
            table = (even, odd)[kind]
            moved = pairs(lambda k, c: (k, table[c]) if table[c] != c else (k ^ 1, c))
            arrays.append(lax.ppermute(arrays[source], AXES, moved))
        return arrays

    def gather_clus(values):
        half = values.shape[0] // 2
        parts = {0: [values]}
        evens = sorted(range(2, clus_count, 2), key=lambda e: bin(e).count("1"))
        for e in evens + list(range(1, clus_count, 2)):
            bits = [1 << b for b in range(clus_count.bit_length()) if e >> b & 1]
            if e & 1:
                parts[e] = [swap(piece, 1) for piece in parts[e ^ 1]]
            elif len(bits) == 2:
                first, second = parts[bits[0]][0], parts[bits[1]][0]
                parts[e] = [swap(first[:half], bits[1]), swap(second[half:], bits[0])]
            else:
                parts[e] = [swap(values, e)]
        return [parts[e] for e in range(clus_count)]

    def per_device(
        density,
        dens_pattern,
        margin_window,
        ovl_pattern,
        keep_mask,
        basis_values,
        rest_density,
        slab_owner,
        cell_lengths,
    ):
        k = lax.axis_index("clus")
        c = lax.axis_index("col")
        rows, cols = dens_pattern.shape
        block = density.shape[0] // rows
        cells = basis_values.shape[2]
        all_blocks = clus_count * rows
        planes, lines, size = rest_density.shape
        devices = clus_count * col_count
        depth = size // devices
        slice_cells = cells // clus_count
        slice_lines = slice_cells // QZ
        patch_lines = cells // QZ
        lines_dev = patch_lines // col_count
        z_start = (size - QZ) // 2
        hartley = cas_table(size)
        hartley_q = jnp.asarray(hartley[z_start : z_start + QZ])
        line_id = np.arange(patch_lines)
        groups = max(1, all_blocks // planes)
        group_size = all_blocks // groups
        y_cells = (
            line_id[None, :] // lines_dev * lines
            + np.arange(groups)[:, None] * lines_dev
            + line_id[None, :] % lines_dev
        )
        fold = 128 // lines
        tiles = planes * lines // 128
        pot_lanes = 2 * rows * patch_lines
        in_kernels = tiles % 16 == 0 and tiles >= depth and groups == 1 and pot_lanes == 128
        row_id = np.arange(size)
        x_of_row = (
            row_id // tiles % clus_count * planes
            + row_id % tiles * fold
            + row_id // (tiles * clus_count)
        )
        forward_x = split_table(hartley[:, x_of_row] * np.float32(1.0 / 256.0))
        inverse_x = split_table(hartley[x_of_row])
        both_y = split_table(hartley)
        line_table = np.zeros((rows, size, pot_lanes), np.float32)
        for b in range(rows):
            for part in range(2):
                start = (part * rows + b) * patch_lines
                line_table[b, :, start : start + patch_lines] = hartley[y_cells[0]].T
        hartley_y = jnp.asarray(hartley[y_cells])
        hartley = jnp.asarray(hartley)

        ratio = cols // rows
        device_id = k * col_count + c
        clus_ids = k ^ jnp.arange(clus_count, dtype=jnp.int32)

        own_phi = lax.dynamic_slice_in_dim(basis_values, k * slice_cells, slice_cells, 2)
        pieces = gather_line(own_phi)

        masked = (
            density.reshape(rows, block, cols, block)
            * dens_pattern.astype(jnp.bfloat16)[:, None, :, None]
        ).reshape(rows * block, cols * block)
        gathered = gather_clus(masked)

        rest_lines = rest_density.reshape(planes * lines, size)
        waves = dot_high("kz,lz->kl", hartley, rest_lines)
        waves = (waves * 256.0).astype(jnp.float16)
        if in_kernels:
            waves = waves.reshape(devices, depth, tiles, 128)
        else:
            waves = waves.reshape(devices, depth, planes * lines)
        moved = exchange(waves)
        if in_kernels:
            plane = forward_planes(
                moved.astype(jnp.float32), forward_x, both_y, clus_count, col_count, lines
            )
        else:
            plane = (
                moved.reshape(clus_count, col_count, depth, planes, lines)
                .transpose(2, 0, 3, 1, 4)
                .reshape(depth, size, size)
                .astype(jnp.float32)
            )
            plane = dot_high("axy,yv->axv", plane, hartley)
            plane = dot_high("ux,axv->auv", hartley * (1.0 / 256.0), plane)

        phi_slice = own_phi.reshape(cols * block, slice_cells)
        margin_masked = (
            margin_window.reshape(cols, block, block)
            * ovl_pattern.astype(jnp.bfloat16)[:, :, None]
        ).reshape(cols * block, block)
        split = 2
        before = lift(clus_ids[:split], phi_slice, margin_masked, gathered[:split], clus_count, 0)
        lifted, window = lift(
            clus_ids[split:], phi_slice, margin_masked, gathered[split:], clus_count, split, before
        )
        where = jnp.asarray(place)[c][clus_ids // ratio]
        *sent, partial_rho = route(clus_ids, where, clus_ids % ratio, lifted, pieces, rows)
        patch_waves = dot_high(
            "qk,lq->kl", hartley_q, partial_rho.reshape(all_blocks * slice_lines, QZ)
        )
        patch_waves = patch_waves.reshape(devices, depth, all_blocks * slice_lines)
        patch_moved = exchange(patch_waves)
        patch_sum = jnp.sum(
            patch_moved.reshape(
                clus_count, col_count, depth, groups, group_size, slice_lines
            ),
            axis=1,
        )
        patch_sum = patch_sum.transpose(2, 3, 1, 0, 4).reshape(
            groups, group_size, depth, patch_lines
        )
        patch_y = dot_high("gizm,gmv->zgiv", patch_sum, hartley_y)
        patch_y = patch_y.reshape(depth, all_blocks, size)
        block_ids = jnp.arange(all_blocks, dtype=jnp.int32)
        x_cells = slab_owner.astype(jnp.int32) * planes + block_ids % planes
        chosen = (x_cells[:, None] == jnp.arange(size, dtype=jnp.int32)[None, :]).astype(jnp.float32)
        hartley_x = jnp.einsum(
            "ix,xu->iu", chosen, hartley, precision=lax.Precision.HIGHEST
        )

        row_parts = []
        for e, part in enumerate(sent):
            row_parts.append(part if e == 0 else swap(part, e))

        factor = green_planes(cell_lengths, size, device_id * depth, depth) * (1.0 / size**3)

        if in_kernels:
            back = inverse_planes(
                plane,
                factor,
                patch_y,
                hartley_x.T,
                hartley_x.reshape(clus_count, rows, size).transpose(1, 0, 2),
                line_table,
                inverse_x,
                both_y,
                tiles,
                clus_count,
                col_count,
                lines,
            )
            back = exchange(back)
            picked = back[:, depth, :depth]
            back = back[:, :depth]
        else:
            plane = (plane + dot_high("iu,ziv->zuv", hartley_x, patch_y)) * factor
            picked = dot_high("iu,zuv->izv", hartley_x, plane).reshape(
                groups, group_size, depth, size
            )
            picked = dot_high("gizv,gmv->gizm", picked, hartley_y).reshape(
                clus_count, rows, depth, patch_lines
            )
            picked = picked.transpose(0, 2, 1, 3).reshape(clus_count, 1, depth, rows * patch_lines)
            leading = lax.reduce_precision(picked, 8, 7)
            picked = jnp.concatenate([leading, picked - leading], axis=-1).astype(jnp.bfloat16)
            picked = jnp.broadcast_to(picked, (clus_count, col_count, depth, pot_lanes))
            picked = picked.reshape(devices, depth, pot_lanes)
            plane = dot_high("xu,auv->axv", hartley, plane)
            plane = dot_high("axv,vy->axy", plane, hartley)
            back = (
                plane.astype(jnp.bfloat16)
                .reshape(depth, clus_count, planes, col_count, lines)
                .transpose(1, 3, 0, 2, 4)
                .reshape(devices, depth, planes * lines)
            )
            back = exchange(jnp.concatenate([back, picked], axis=-1))
            picked = back[:, :, planes * lines :]
            back = back[:, :, : planes * lines]
        picked = picked.astype(jnp.float32).reshape(size, 2, rows, patch_lines)
        patch_pot = dot_high("krm,qk->rmq", picked[:, 0] + picked[:, 1], hartley_q)
        patch_pot = patch_pot.reshape(rows, cells)
        back = back.reshape(size, planes * lines).astype(jnp.float32)
        potential = dot_high("kl,kz->lz", back, hartley).reshape(planes, lines, size)

        hartree = hartree_product(
            clus_ids,
            dens_pattern,
            patch_pot,
            basis_values.reshape(cols * block, cells),
            row_parts,
        )

        span = clus_count // col_count
        window = (window * 32.0).astype(jnp.float16)
        arrived = []
        for e in range(clus_count):
            arrived.append(swap(window[e], e) if e else window[e])
        arrived = jnp.stack(arrived)
        window = jnp.stack(
            [lax.dynamic_index_in_dim(arrived, k ^ b, 0, keepdims=False) for b in range(clus_count)]
        ).reshape(col_count, span, block, block)
        summed = 0.0
        for step in range(col_count):
            part = lax.dynamic_index_in_dim(window, c ^ step, 0, keepdims=False)
            if step:
                part = lax.ppermute(part, AXES, pairs(lambda k, c: (k, c ^ step)))
            summed = summed + part.astype(jnp.float32)
        summed = summed * (keep_mask.astype(jnp.float32)[0][:, None, None] * (1.0 / 32.0))
        product = summed.transpose(1, 0, 2).reshape(block, span * block).astype(jnp.bfloat16)
        return (potential, hartree, product)

    return per_device


def solution(mesh):
    in_specs = (
        P("clus", "col"),
        P("clus", "col"),
        P("col", "clus"),
        P("col", "clus"),
        P("clus", "col"),
        P("col", None, None),
        P("clus", "col", None),
        P(),
        P(),
    )
    out_specs = (P("clus", "col", None), P("clus", "col"), P("clus", "col"))
    clus_count, col_count = mesh.shape["clus"], mesh.shape["col"]
    return jax.shard_map(
        make_program(clus_count, col_count),
        mesh=mesh,
        in_specs=in_specs,
        out_specs=out_specs,
        check_vma=False,
    )
```
